32 devices in a mesh: seq: 8 (over z, x), dp: 4 (over y, core).
Axes of the slice: x: 2, y: 2, z: 4, core: 2. Of those that a mesh axis runs over, the one named last changes fastest.
Arguments:
- features: bfloat16 [4, 2048, 2048], P('dp', 'seq'), may hold values from -6 to 6
- key_proj: bfloat16 [4, 2048, 128], P('dp', 'seq'), may hold values from -6 to 6
- query_proj: bfloat16 [4, 2048, 128], P('dp', 'seq'), may hold values from -6 to 6
- log_decay: float32 [4, 32, 2048], P('dp', None, 'seq'), may hold values from -0.002 to 0
- doc_start: int32 [4, 2048], P('dp', 'seq'), may hold values from 0 to 1, as said below
- loss_weight: float32 [4, 2048], P('dp', 'seq'), may hold values from 0.25 to 6
- target: bfloat16 [4, 2048, 2048], P('dp', 'seq'), may hold values from -6 to 6
Outputs:
- outputs: bfloat16 [4, 2048, 2048], P('dp', 'seq')
- grad_features: bfloat16 [4, 2048, 2048], P('dp', 'seq')
- grad_keys: bfloat16 [4, 2048, 128], P('dp', 'seq')
- grad_queries: bfloat16 [4, 2048, 128], P('dp', 'seq')
- grad_decay: float32 [4, 32, 2048], P('dp', None, 'seq')
The draws below stay inside these ranges and needn't reach their ends.
Inputs may be any that keep to these rules, and one draw needn't show every extreme that they name: `doc_start`: position 0 of every row begins a document; a document runs from its 1 to the next 1 or the row's end and holds at most 1024 tokens; every row holds one of exactly 1024.
All inputs are finite; a program needn't handle non-finite values.
Results may differ from the reference program's by a relative error of at most 0.0085.
Values sent between devices are 32-bit elements; how exact they have to be, the bound alone decides.
A program may use at most 64 MiB of HBM per device.

```python
import math
import jax
import jax.numpy as jnp
from jax import lax

H = 32
P_SIZE = 64
N = 128
BLOCK = 256
TOK_SEQ = 256
ROWS = 4
SEQ_LEN = 2048
DOC_MOST = 1024


def draw_log_decay(key, part):
    key_rate, key_rough, key_block = jax.random.split(key, 3)
    low_end = math.log(2e-05)
    high_end = math.log(0.001)
    head_rate = jnp.exp(jax.random.uniform(key_rate, (ROWS, H, 1), jnp.float32, low_end, high_end))
    roughness = jax.random.uniform(key_rough, (ROWS, H, SEQ_LEN), jnp.float32, 1.0, 2.0)
    shards = SEQ_LEN // TOK_SEQ
    block_scale = jax.random.uniform(key_block, (ROWS, H, shards, 1), jnp.float32, 0.5, 1.0)
    block_scale = jnp.broadcast_to(block_scale, (ROWS, H, shards, TOK_SEQ)).reshape(ROWS, H, SEQ_LEN)
    return -head_rate * roughness * block_scale


def draw_doc_start(key, part):
    row_keys = jax.random.split(key, ROWS)

    def one_row(row_key):
        key_len, key_pick = jax.random.split(row_key)
        lengths = jax.random.randint(key_len, (SEQ_LEN,), 1, DOC_MOST + 1)
        chosen = jax.random.randint(key_pick, (), 0, 2)
        lengths = jnp.where(jnp.arange(SEQ_LEN) == chosen, DOC_MOST, lengths)
        offsets = jnp.cumsum(lengths) - lengths
        return jnp.zeros((SEQ_LEN,), jnp.int32).at[offsets].set(1, mode='drop')
    return jax.vmap(one_row)(row_keys)


def draw_loss_weight(key, part):
    position = jnp.arange(SEQ_LEN, dtype=jnp.float32)[None, :] / SEQ_LEN
    row_share = jnp.arange(ROWS, dtype=jnp.float32)[:, None] / ROWS
    rising = 1.0 + position + row_share
    base_weight = jax.random.uniform(key, (ROWS, SEQ_LEN), jnp.float32, 0.5, 1.5)
    return base_weight * rising


def steps_of(stream_key, dims, cuts, least, largest):
    loudness = 1.0
    for dim, parts in cuts:
        steps = jax.random.uniform(jax.random.fold_in(jax.random.fold_in(stream_key, 6), dim), (parts,), jnp.float32, least / len(cuts), largest / len(cuts))
        loudness = loudness * jnp.repeat(jnp.exp(steps), dims[dim] // parts).reshape((-1,) + (1,) * (len(dims) - 1 - dim))
    return loudness


def centred(own_key, extent, spread, limit, cuts=(), held_as=jnp.bfloat16):
    result = spread * jax.random.normal(own_key, extent, jnp.float32)
    if cuts:
        result = result * steps_of(own_key, extent, cuts, -0.22, 0.18)
    return jnp.clip(result, -limit, limit).astype(held_as)


def setup_inputs(seed: int = 0) -> dict:
    key_of = jax.random.split(jax.random.key(seed), 8)
    features = centred(key_of[0], (ROWS, SEQ_LEN, H * P_SIZE), 1.0, 6.0, ((0, 4), (1, 8)))
    key_proj = centred(key_of[1], (ROWS, SEQ_LEN, N), 1.0, 6.0, ((0, 4), (1, 8)))
    query_proj = centred(key_of[2], (ROWS, SEQ_LEN, N), 1.0, 6.0, ((0, 4), (1, 8)))
    log_decay = draw_log_decay(jax.random.fold_in(key_of[7], 71), 0)
    doc_start = draw_doc_start(jax.random.fold_in(key_of[7], 71), 0)
    loss_weight = draw_loss_weight(jax.random.fold_in(key_of[7], 71), 0)
    target = centred(key_of[6], (ROWS, SEQ_LEN, H * P_SIZE), 1.0, 6.0, ((0, 4), (1, 8)))
    return dict(features=features, key_proj=key_proj, query_proj=query_proj, log_decay=log_decay, doc_start=doc_start, loss_weight=loss_weight, target=target)


exact_mode = lax.Precision.HIGHEST

def block_tail(values, key_rows, running, segment):
    last_segment = segment[-1]
    tail_weight = jnp.where(segment[None, :] == last_segment, jnp.exp(running[:, -1:] - running), 0.0)
    fresh = jnp.einsum('sn,shp->hpn', key_rows, values * tail_weight.T[:, :, None], precision=exact_mode)
    keep_gain = jnp.exp(running[:, -1]) * (last_segment == 0).astype(jnp.float32)
    return (fresh, keep_gain)

def unpack(feature, key_in, decay_log, starts, key_scale):
    heads = decay_log.shape[0]
    length = feature.shape[0]
    values = feature.astype(jnp.float32).reshape(length, heads, feature.shape[1] // heads)
    key_rows = key_in.astype(jnp.float32) * key_scale
    running = jnp.cumsum(decay_log, axis=1)
    segment = jnp.cumsum(starts)
    return (values, key_rows, running, segment)

def block_step(carry_state, block_piece, key_scale):
    feature, key_in, query_in, decay_log, starts = block_piece
    values, key_rows, running, segment = unpack(feature, key_in, decay_log, starts, key_scale)
    query_rows = query_in.astype(jnp.float32)
    length = values.shape[0]
    position = jnp.arange(length)
    linked = (position[:, None] >= position[None, :]) & (segment[:, None] == segment[None, :])
    scores = jnp.dot(query_in, key_in.T, preferred_element_type=jnp.float32) * key_scale
    mixing = jnp.where(linked, scores, 0.0).astype(jnp.bfloat16)
    mixing = lax.optimization_barrier(mixing)
    lifted = (values * jnp.exp(-running).T[:, :, None]).astype(jnp.bfloat16).reshape(length, -1)
    lifted = lax.optimization_barrier(lifted)
    rise = jnp.exp(running).T
    inner_part = jnp.dot(mixing, lifted, preferred_element_type=jnp.float32).reshape(values.shape) * rise[:, :, None]
    opened = (segment == 0).astype(jnp.float32)
    entry_gain = rise * opened[:, None]
    carried = jnp.einsum('tn,hpn->thp', query_rows, carry_state, precision=exact_mode) * entry_gain[:, :, None]
    fresh, keep_gain = block_tail(values, key_rows, running, segment)
    new_state = keep_gain[:, None, None] * carry_state + fresh
    return (new_state, (inner_part + carried).reshape(length, -1))

def split_blocks(feature, key_in, query_in, decay_log, starts):
    blocks = feature.shape[0] // BLOCK
    heads = decay_log.shape[0]
    return (feature.reshape(blocks, BLOCK, feature.shape[1]), key_in.reshape(blocks, BLOCK, key_in.shape[1]), query_in.reshape(blocks, BLOCK, query_in.shape[1]), decay_log.reshape(heads, blocks, BLOCK).transpose(1, 0, 2), starts.reshape(blocks, BLOCK))

def process(feature, key_in, query_in, decay_log, starts, carry_state):
    key_scale = 1.0 / math.sqrt(key_in.shape[1] * BLOCK)
    pieces = split_blocks(feature, key_in, query_in, decay_log, starts)

    def advance(current, block_piece):
        return block_step(current, block_piece, key_scale)
    final_state, results = lax.scan(advance, carry_state, pieces)
    return (results.reshape(feature.shape[0], feature.shape[1]), final_state)

def reference(features, key_proj, query_proj, log_decay, doc_start, loss_weight, target):
    mean_weight = jnp.mean(loss_weight)

    def one_row(row_pieces):
        feature, key_in, query_in, decay_log, starts, weight, target_row = row_pieces
        empty_state = jnp.zeros((H, P_SIZE, N), jnp.float32)

        def forward(first, second, third, fourth):
            return process(first, second, third, fourth, starts, empty_state)[0]
        output, pullback = jax.vjp(forward, feature, key_in, query_in, decay_log)
        grad_out = (weight / mean_weight)[:, None] * (output - target_row.astype(jnp.float32))
        gradients = pullback(grad_out)
        return (output.astype(jnp.bfloat16), gradients[0], gradients[1], gradients[2], gradients[3])
    results = lax.map(one_row, (features, key_proj, query_proj, log_decay, doc_start, loss_weight, target))
    return (results[0], results[1], results[2], results[3], results[4])
```

```python
import functools
import math

import jax
import jax.numpy as jnp
from jax import lax
from jax.experimental import pallas as pl
from jax.experimental.pallas import tpu as pltpu
from jax.sharding import PartitionSpec as P

F32 = jnp.float32
BF16 = jnp.bfloat16
MESH = pl.DeviceIdType.MESH
CHUNK = 256
EXTRA = 8


def mm(a, b):
    return jnp.dot(a, b, preferred_element_type=F32)


def mm_nt(a, b):
    return lax.dot_general(a, b, (((1,), (1,)), ((), ())), preferred_element_type=F32)


def split(x):
    hi = x.astype(BF16)
    lo = (x - hi.astype(F32)).astype(BF16)
    return hi, lo


def kernel(
    n_seq, n_dp, heads,
    f_ref, k_ref, q_ref, ld_ref, ds_ref, w_ref, t_ref,
    out_ref, gf_ref, gk_ref, gq_ref, gd_ref,
    xf_send, xf_recv, zf_send, zf_recv, xb_send, xb_recv, zb_send, zb_recv,
    rise_s, inv_s, y_s, dl_s, lift_s, so_s,
    dmix_s, dmixt_s, dq_s, dk_s, rt_s, ex_s,
    wown, wseq, wrow, wdp,
    xfs, xfr, zfs, zfr, xbs, xbr, zbs, zbr, wss, wsr, wds, wdr,
):
    length, width = f_ref.shape
    state = k_ref.shape[1]
    head_size = width // heads
    chunks = width // CHUNK
    per_chunk = CHUNK // head_size
    sigma = 1.0 / math.sqrt(state * length)

    me = lax.axis_index("seq")
    row = lax.axis_index("dp")
    pair = me // 2
    pairs = n_seq // 2
    is_odd = me % 2
    odd = is_odd == 1
    partner = me + 1 - 2 * is_odd

    barrier = pltpu.get_barrier_semaphore()

    def greet_seq(d, _):
        pl.semaphore_signal(
            barrier, inc=1, device_id={"seq": (me + d) % n_seq}, device_id_type=MESH
        )
        return 0

    def greet_dp(d, _):
        pl.semaphore_signal(
            barrier, inc=1, device_id={"dp": (row + d) % n_dp}, device_id_type=MESH
        )
        return 0

    lax.fori_loop(1, n_seq, greet_seq, 0)
    lax.fori_loop(1, n_dp, greet_dp, 0)

    wown[...] = jnp.broadcast_to(jnp.sum(w_ref[...], axis=1, keepdims=True), wown.shape)

    starts = ds_ref[...].astype(F32)
    table = jnp.concatenate(
        [
            ld_ref[...],
            jnp.broadcast_to(starts, (8, length)),
            jnp.broadcast_to(w_ref[...], (8, length)),
            jnp.zeros((128 - heads - 16, length), F32),
        ],
        axis=0,
    )
    rows_i = lax.broadcasted_iota(jnp.int32, (length, length), 0)
    cols_i = lax.broadcasted_iota(jnp.int32, (length, length), 1)
    lower = (rows_i >= cols_i).astype(F32).astype(BF16)
    upper = (rows_i <= cols_i).astype(F32).astype(BF16)
    eye = (rows_i == cols_i).astype(F32).astype(BF16)
    eye_n = eye[:state, :state]
    table_hi, table_lo = split(table)
    cumulative = mm_nt(lower, table_hi) + mm_nt(lower, table_lo)
    turned = mm_nt(eye, table_hi) + mm_nt(eye, table_lo)
    seg_col = cumulative[:, heads:heads + 1]
    seg_row = mm(jnp.broadcast_to(starts, (8, length)).astype(BF16), upper)[0:1]
    last_seg = jnp.sum(starts, axis=1, keepdims=True)
    tail_row = (seg_row == last_seg).astype(F32)
    tail_col = (seg_col == last_seg).astype(F32)
    open_row = (seg_row == 0.0).astype(F32)
    open_col = (seg_col == 0.0).astype(F32)
    whole_block = (last_seg == 0.0).astype(F32)
    run_hi, run_lo = split(cumulative)

    keys = k_ref[...]
    queries = q_ref[...]
    keys_t = (mm_nt(eye_n, keys) * tail_row).astype(BF16)
    queries_t = (mm_nt(eye_n, queries) * open_row).astype(BF16)
    keys_tail = (keys.astype(F32) * tail_col).astype(BF16)
    queries_open = (queries.astype(F32) * open_col).astype(BF16)

    head_i = lax.broadcasted_iota(jnp.int32, (128, CHUNK), 0)
    lane_h = lax.broadcasted_iota(jnp.int32, (128, CHUNK), 1) // head_size

    def spread(c):
        return (head_i == lane_h + c * per_chunk).astype(F32).astype(BF16)

    def lanes(c):
        return pl.ds(pl.multiple_of(c * CHUNK, CHUNK), CHUNK)

    def to_partner(send, recv, ss, rs, c):
        return pltpu.make_async_remote_copy(
            src_ref=send.at[c], dst_ref=recv.at[c], send_sem=ss.at[c], recv_sem=rs.at[c],
            device_id={"seq": partner}, device_id_type=MESH,
        )

    def to_pair(send, recv, ss, rs, c, target):
        return pltpu.make_async_remote_copy(
            src_ref=send.at[c], dst_ref=recv.at[c], send_sem=ss.at[c], recv_sem=rs.at[c],
            device_id={"seq": target}, device_id_type=MESH,
        )

    def w_seq(d):
        return pltpu.make_async_remote_copy(
            src_ref=wown, dst_ref=wseq.at[d - 1], send_sem=wss.at[d - 1], recv_sem=wsr.at[d - 1],
            device_id={"seq": (me + d) % n_seq}, device_id_type=MESH,
        )

    def w_dp(d):
        return pltpu.make_async_remote_copy(
            src_ref=wrow, dst_ref=wdp.at[d - 1], send_sem=wds.at[d - 1], recv_sem=wdr.at[d - 1],
            device_id={"dp": (row + d) % n_dp}, device_id_type=MESH,
        )

    pl.semaphore_wait(barrier, n_seq + n_dp - 2)

    def start_w(d, _):
        w_seq(d).start()
        return 0

    def fresh_step(c, _):
        e = spread(c)
        run_x = mm(run_hi, e) + mm(run_lo, e)
        rise = jnp.exp(run_x)
        inv = jnp.exp(-run_x)
        lifted = (f_ref[:, lanes(c)].astype(F32) * inv).astype(BF16)
        gain = rise[length - 1:length]
        xf_send[c, 0:state, :] = mm(keys_t, lifted) * (gain * sigma)
        xf_send[c, state:state + EXTRA, :] = jnp.broadcast_to(gain * whole_block, (EXTRA, CHUNK))
        to_partner(xf_send, xf_recv, xfs, xfr, c).start()
        rise_s[c] = rise
        inv_s[c] = inv
        lift_s[c] = lifted
        return 0

    lax.fori_loop(0, chunks, fresh_step, 0)
    lax.fori_loop(1, n_seq, start_w, 0)

    linked = (rows_i >= cols_i) & (seg_col == seg_row)
    linked_t = (rows_i <= cols_i) & (seg_col == seg_row)
    mixing = jnp.where(linked, mm_nt(queries, keys) * sigma, 0.0).astype(BF16)
    mixing_t = jnp.where(linked_t, mm_nt(keys, queries) * sigma, 0.0).astype(BF16)

    @pl.when(pair == 0)
    def _():
        zf_recv[...] = jnp.zeros_like(zf_recv)

    @pl.when(pair == pairs - 1)
    def _():
        zb_recv[...] = jnp.zeros_like(zb_recv)

    dmix_s[...] = jnp.zeros_like(dmix_s)
    dmixt_s[...] = jnp.zeros_like(dmixt_s)
    dq_s[...] = jnp.zeros_like(dq_s)
    dk_s[...] = jnp.zeros_like(dk_s)
    rt_s[...] = jnp.zeros_like(rt_s)
    ex_s[...] = jnp.zeros_like(ex_s)

    def inner_step(c, _):
        y_s[c] = mm(mixing, lift_s[c])
        return 0

    def add_w(d, total):
        w_seq(d).wait_recv()
        return total + wseq[d - 1]

    wrow[...] = lax.fori_loop(1, n_seq, add_w, wown[...])

    def start_d(d, _):
        w_dp(d).start()
        return 0

    lax.fori_loop(1, n_dp, start_d, 0)
    lax.fori_loop(0, chunks, inner_step, 0)

    def add_d(d, total):
        w_dp(d).wait_recv()
        return total + wdp[d - 1]

    total = lax.fori_loop(1, n_dp, add_d, wrow[...])
    mean_weight = total[0:1, 0:1] * (1.0 / (length * n_seq * n_dp))
    weight = turned[:, heads + 8:heads + 9] / mean_weight

    def forward_step(c, _):
        to_partner(xf_send, xf_recv, xfs, xfr, c).wait_recv()

        @pl.when(pair > 0)
        def _():
            to_pair(zf_send, zf_recv, zfs, zfr, c, me).wait_recv()

        own = xf_send[c, 0:state, :]
        own_keep = xf_send[c, state:state + 1, :]
        other = xf_recv[c, 0:state, :]
        other_keep = xf_recv[c, state:state + 1, :]
        entry = zf_recv[c]
        before = jnp.where(odd, other + other_keep * entry, entry)
        after = own + own_keep * before
        zf_send[c] = jnp.where(odd, after, other + other_keep * after)

        @pl.when(pair < pairs - 1)
        def _():
            to_pair(zf_send, zf_recv, zfs, zfr, c, me + 2).start()

        so_s[c] = after
        before_h = before.astype(BF16)
        rise = rise_s[c]
        y = rise * (y_s[c] + mm(queries_open, before_h))
        out_ref[:, lanes(c)] = y.astype(BF16)
        grad = weight * (y - t_ref[:, lanes(c)].astype(F32))
        z = (grad * rise).astype(BF16)
        xb_send[c] = mm(queries_t, z)
        to_partner(xb_send, xb_recv, xbs, xbr, c).start()
        y_s[c] = grad * y
        dq_s[...] += mm_nt(z, before_h)
        lifted = lift_s[c]
        dmix_s[...] += mm_nt(z, lifted)
        dmixt_s[...] += mm_nt(lifted, z)
        dl_s[c] = mm(mixing_t, z)
        return 0

    lax.fori_loop(0, chunks, forward_step, 0)

    def backward_step(c, _):
        to_partner(xb_send, xb_recv, xbs, xbr, c).wait_recv()

        @pl.when(pair < pairs - 1)
        def _():
            to_pair(zb_send, zb_recv, zbs, zbr, c, me).wait_recv()

        own = xb_send[c]
        own_keep = xf_send[c, state:state + 1, :]
        other = xb_recv[c]
        other_keep = xf_recv[c, state:state + 1, :]
        entry = zb_recv[c]
        adjoint = jnp.where(odd, entry, other + other_keep * entry)
        onward = own + own_keep * adjoint
        zb_send[c] = jnp.where(odd, other + other_keep * onward, onward)

        @pl.when(pair > 0)
        def _():
            to_pair(zb_send, zb_recv, zbs, zbr, c, me - 2).start()

        e = spread(c)
        gain = rise_s[c, length - 1:length, :]
        scaled = (adjoint * (gain * sigma)).astype(BF16)
        d_feature = inv_s[c] * (dl_s[c] + mm(keys_tail, scaled))
        gf_ref[:, lanes(c)] = d_feature.astype(BF16)
        change = y_s[c] - f_ref[:, lanes(c)].astype(F32) * d_feature
        change_hi, change_lo = split(change)
        rt_s[...] += mm_nt(e, change_hi) + mm_nt(e, change_lo)
        dk_s[...] += mm_nt(lift_s[c], scaled)
        end_hi, end_lo = split(adjoint * so_s[c])
        ex_s[...] += mm_nt(e, end_hi) + mm_nt(e, end_lo)
        return 0

    lax.fori_loop(0, chunks, backward_step, 0)

    d_scores = (jnp.where(linked, dmix_s[...], 0.0) * sigma).astype(BF16)
    d_scores_t = (jnp.where(linked_t, dmixt_s[...], 0.0) * sigma).astype(BF16)
    gq_ref[...] = (mm(d_scores, keys) + open_col * dq_s[...]).astype(BF16)
    gk_ref[...] = (mm(d_scores_t, queries) + tail_col * dk_s[...]).astype(BF16)
    rt_hi, rt_lo = split(rt_s[...])
    decay = mm(rt_hi, lower) + mm(rt_lo, lower) + jnp.sum(ex_s[...], axis=1, keepdims=True)
    gd_ref[...] = decay[:heads]

    def finish_step(c, _):
        to_partner(xf_send, xf_recv, xfs, xfr, c).wait_send()
        to_partner(xb_send, xb_recv, xbs, xbr, c).wait_send()

        @pl.when(pair < pairs - 1)
        def _():
            to_pair(zf_send, zf_recv, zfs, zfr, c, me + 2).wait_send()

        @pl.when(pair > 0)
        def _():
            to_pair(zb_send, zb_recv, zbs, zbr, c, me - 2).wait_send()

        return 0

    lax.fori_loop(0, chunks, finish_step, 0)

    def finish_w(d, _):
        w_seq(d).wait_send()
        return 0

    def finish_d(d, _):
        w_dp(d).wait_send()
        return 0

    lax.fori_loop(1, n_seq, finish_w, 0)
    lax.fori_loop(1, n_dp, finish_d, 0)


def body(features, key_proj, query_proj, log_decay, doc_start, loss_weight, target):
    n_seq, n_dp = lax.axis_size("seq"), lax.axis_size("dp")
    length, width = features.shape[1:]
    state = key_proj.shape[2]
    heads = log_decay.shape[1]
    chunks = width // CHUNK
    vmem = pl.BlockSpec(memory_space=pltpu.VMEM)
    big = (chunks, length, CHUNK)
    small = (chunks, state, CHUNK)
    padded = (chunks, state + EXTRA, CHUNK)
    scratch = [
        pltpu.VMEM(padded, F32), pltpu.VMEM(padded, F32),
        pltpu.VMEM(small, F32), pltpu.VMEM(small, F32),
        pltpu.VMEM(small, F32), pltpu.VMEM(small, F32),
        pltpu.VMEM(small, F32), pltpu.VMEM(small, F32),
        pltpu.VMEM(big, F32), pltpu.VMEM(big, F32), pltpu.VMEM(big, F32), pltpu.VMEM(big, F32),
        pltpu.VMEM(big, BF16), pltpu.VMEM(small, F32),
        pltpu.VMEM((length, length), F32), pltpu.VMEM((length, length), F32),
        pltpu.VMEM((length, state), F32), pltpu.VMEM((length, state), F32),
        pltpu.VMEM((128, length), F32), pltpu.VMEM((128, state), F32),
        pltpu.VMEM((8, 128), F32), pltpu.VMEM((n_seq - 1, 8, 128), F32),
        pltpu.VMEM((8, 128), F32), pltpu.VMEM((n_dp - 1, 8, 128), F32),
    ]
    scratch += [pltpu.SemaphoreType.DMA((chunks,))] * 8
    scratch += [pltpu.SemaphoreType.DMA((n_seq - 1,))] * 2
    scratch += [pltpu.SemaphoreType.DMA((n_dp - 1,))] * 2
    results = pl.pallas_call(
        functools.partial(kernel, n_seq, n_dp, heads),
        out_shape=(
            jax.ShapeDtypeStruct((length, width), BF16),
            jax.ShapeDtypeStruct((length, width), BF16),
            jax.ShapeDtypeStruct((length, state), BF16),
            jax.ShapeDtypeStruct((length, state), BF16),
            jax.ShapeDtypeStruct((heads, length), F32),
        ),
        in_specs=[vmem] * 7,
        out_specs=(vmem,) * 5,
        scratch_shapes=scratch,
        compiler_params=pltpu.CompilerParams(
            collective_id=0, has_side_effects=True, vmem_limit_bytes=48 << 20
        ),
        name="mixing",
    )(
        features[0], key_proj[0], query_proj[0], log_decay[0], doc_start, loss_weight, target[0]
    )
    return tuple(r[None] for r in results)


def solution(mesh):
    placed = (
        P("dp", "seq", None),
        P("dp", "seq", None),
        P("dp", "seq", None),
        P("dp", None, "seq"),
        P("dp", "seq"),
        P("dp", "seq"),
        P("dp", "seq", None),
    )
    return jax.shard_map(
        body,
        mesh=mesh,
        in_specs=placed,
        out_specs=(
            P("dp", "seq", None),
            P("dp", "seq", None),
            P("dp", "seq", None),
            P("dp", "seq", None),
            P("dp", None, "seq"),
        ),
        check_vma=False,
    )
```

```python
import functools
import math

import jax
import jax.numpy as jnp
from jax import lax
from jax.experimental import pallas as pl
from jax.experimental.pallas import tpu as pltpu
from jax.sharding import PartitionSpec as P

F32 = jnp.float32
BF16 = jnp.bfloat16
MESH = pl.DeviceIdType.MESH
CHUNK = 128
EXTRA = 8
LAG_LAST = 2
LAG_PAIR = 5


def mm(a, b):
    return jnp.dot(a, b, preferred_element_type=F32)


def mm_nt(a, b):
    return lax.dot_general(a, b, (((1,), (1,)), ((), ())), preferred_element_type=F32)


def split(x):
    hi = x.astype(BF16)
    lo = (x - hi.astype(F32)).astype(BF16)
    return hi, lo


def kernel(
    n_seq, n_dp, heads,
    f_hbm, k_hbm, q_hbm, ld_hbm, ds_hbm, w_hbm, t_hbm,
    out_ref, gf_ref, gk_ref, gq_ref, gd_ref,
    xf_send, xf_recv, zf_send, zf_recv, xb_send, xb_recv, zb_send, zb_recv,
    rise_s, inv_s, y_s, dl_s, lift_s, so_s,
    dmix_s, dmixt_s, dq_s, dk_s, gk_s, rt_s, ex_s,
    wown, wseq, wrow, wdp,
    f_ref, k_ref, q_ref, ld_ref, ds_ref, w_ref, t_ref, in_sem,
    xfs, xfr, zfs, zfr, xbs, xbr, zbs, zbr, wss, wsr, wds, wdr,
):
    length, width = f_ref.shape
    state = k_ref.shape[1]
    head_size = width // heads
    chunks = width // CHUNK
    per_chunk = CHUNK // head_size
    sigma = 1.0 / math.sqrt(state * length)

    me = lax.axis_index("seq")
    row = lax.axis_index("dp")
    pair = me // 2
    pairs = n_seq // 2
    is_odd = me % 2
    odd = is_odd == 1
    partner = me + 1 - 2 * is_odd

    fetches = [
        pltpu.make_async_copy(src, dst, in_sem.at[i])
        for i, (src, dst) in enumerate(
            [
                (ld_hbm, ld_ref), (ds_hbm, ds_ref), (w_hbm, w_ref), (k_hbm, k_ref),
                (q_hbm, q_ref), (f_hbm, f_ref), (t_hbm, t_ref),
            ]
        )
    ]
    for fetch in fetches:
        fetch.start()
    barrier = pltpu.get_barrier_semaphore()

    def greet_seq(d, _):
        pl.semaphore_signal(
            barrier, inc=1, device_id={"seq": (me + d) % n_seq}, device_id_type=MESH
        )
        return 0

    def greet_dp(d, _):
        pl.semaphore_signal(
            barrier, inc=1, device_id={"dp": (row + d) % n_dp}, device_id_type=MESH
        )
        return 0

    lax.fori_loop(1, n_seq, greet_seq, 0)
    lax.fori_loop(1, n_dp, greet_dp, 0)

    for fetch in fetches[:5]:
        fetch.wait()
    wown[...] = jnp.broadcast_to(jnp.sum(w_ref[...], axis=1, keepdims=True), wown.shape)

    starts = ds_ref[...].astype(F32)
    table = jnp.concatenate(
        [
            ld_ref[...],
            jnp.broadcast_to(starts, (8, length)),
            jnp.broadcast_to(w_ref[...], (8, length)),
            jnp.zeros((128 - heads - 16, length), F32),
        ],
        axis=0,
    )
    rows_i = lax.broadcasted_iota(jnp.int32, (length, length), 0)
    cols_i = lax.broadcasted_iota(jnp.int32, (length, length), 1)
    lower = (rows_i >= cols_i).astype(F32).astype(BF16)
    upper = (rows_i <= cols_i).astype(F32).astype(BF16)
    eye = (rows_i == cols_i).astype(F32).astype(BF16)
    eye_n = eye[:state, :state]
    table_hi, table_lo = split(table)
    cumulative = mm_nt(lower, table_hi) + mm_nt(lower, table_lo)
    turned = mm_nt(eye, table_hi) + mm_nt(eye, table_lo)
    seg_col = cumulative[:, heads:heads + 1]
    seg_row = mm(jnp.broadcast_to(starts, (8, length)).astype(BF16), upper)[0:1]
    last_seg = jnp.sum(starts, axis=1, keepdims=True)
    tail_row = (seg_row == last_seg).astype(F32)
    tail_col = (seg_col == last_seg).astype(F32)
    open_row = (seg_row == 0.0).astype(F32)
    open_col = (seg_col == 0.0).astype(F32)
    whole_block = (last_seg == 0.0).astype(F32)
    run_hi, run_lo = split(cumulative)

    keys = k_ref[...]
    queries = q_ref[...]
    keys_t = (mm_nt(eye_n, keys) * tail_row).astype(BF16)
    queries_t = (mm_nt(eye_n, queries) * open_row).astype(BF16)
    keys_tail = (keys.astype(F32) * tail_col).astype(BF16)
    queries_open = (queries.astype(F32) * open_col).astype(BF16)

    head_i = lax.broadcasted_iota(jnp.int32, (128, CHUNK), 0)
    lane_h = lax.broadcasted_iota(jnp.int32, (128, CHUNK), 1) // head_size

    def spread(c):
        return (head_i == lane_h + c * per_chunk).astype(F32).astype(BF16)

    def lanes(c):
        return pl.ds(pl.multiple_of(c * CHUNK, CHUNK), CHUNK)

    def to_partner(send, recv, ss, rs, c):
        return pltpu.make_async_remote_copy(
            src_ref=send.at[c], dst_ref=recv.at[c], send_sem=ss.at[c], recv_sem=rs.at[c],
            device_id={"seq": partner}, device_id_type=MESH,
        )

    def to_pair(send, recv, ss, rs, c, target):
        return pltpu.make_async_remote_copy(
            src_ref=send.at[c], dst_ref=recv.at[c], send_sem=ss.at[c], recv_sem=rs.at[c],
            device_id={"seq": target}, device_id_type=MESH,
        )

    def w_seq(d):
        return pltpu.make_async_remote_copy(
            src_ref=wown, dst_ref=wseq.at[d - 1], send_sem=wss.at[d - 1], recv_sem=wsr.at[d - 1],
            device_id={"seq": (me + d) % n_seq}, device_id_type=MESH,
        )

    def w_dp(d):
        return pltpu.make_async_remote_copy(
            src_ref=wrow, dst_ref=wdp.at[d - 1], send_sem=wds.at[d - 1], recv_sem=wdr.at[d - 1],
            device_id={"dp": (row + d) % n_dp}, device_id_type=MESH,
        )

    pl.semaphore_wait(barrier, n_seq + n_dp - 2)

    def start_w(d, _):
        w_seq(d).start()
        return 0

    def fresh_step(c, _):
        e = spread(c)
        run_x = mm(run_hi, e) + mm(run_lo, e)
        rise = jnp.exp(run_x)
        inv = jnp.exp(-run_x)
        lifted = (f_ref[:, lanes(c)].astype(F32) * inv).astype(BF16)
        gain = rise[length - 1:length]
        xf_send[c, 0:state, :] = mm(keys_t, lifted) * (gain * sigma)
        xf_send[c, state:state + EXTRA, :] = jnp.broadcast_to(gain * whole_block, (EXTRA, CHUNK))
        to_partner(xf_send, xf_recv, xfs, xfr, c).start()
        rise_s[c] = rise
        inv_s[c] = inv
        lift_s[c] = lifted
        return 0

    lax.fori_loop(1, n_seq, start_w, 0)
    fetches[5].wait()
    first = chunks // 4
    lax.fori_loop(0, first, fresh_step, 0)

    def add_w(d, total):
        w_seq(d).wait_recv()
        return total + wseq[d - 1]

    wrow[...] = lax.fori_loop(1, n_seq, add_w, wown[...])

    def start_d(d, _):
        w_dp(d).start()
        return 0

    lax.fori_loop(1, n_dp, start_d, 0)
    lax.fori_loop(first, chunks, fresh_step, 0)

    linked = (rows_i >= cols_i) & (seg_col == seg_row)
    linked_t = (rows_i <= cols_i) & (seg_col == seg_row)
    mixing = jnp.where(linked, mm_nt(queries, keys) * sigma, 0.0).astype(BF16)
    mixing_t = jnp.where(linked_t, mm_nt(keys, queries) * sigma, 0.0).astype(BF16)

    @pl.when(pair == 0)
    def _():
        zf_recv[...] = jnp.zeros_like(zf_recv)

    @pl.when(pair == pairs - 1)
    def _():
        zb_recv[...] = jnp.zeros_like(zb_recv)

    dmix_s[...] = jnp.zeros_like(dmix_s)
    dmixt_s[...] = jnp.zeros_like(dmixt_s)
    dq_s[...] = jnp.zeros_like(dq_s)
    dk_s[...] = jnp.zeros_like(dk_s)
    rt_s[...] = jnp.zeros_like(rt_s)
    ex_s[...] = jnp.zeros_like(ex_s)

    def inner_step(c, _):
        y_s[c] = mm(mixing, lift_s[c])
        return 0

    lax.fori_loop(0, chunks, inner_step, 0)

    def add_d(d, total):
        w_dp(d).wait_recv()
        return total + wdp[d - 1]

    total = lax.fori_loop(1, n_dp, add_d, wrow[...])
    over_mean = (length * n_seq * n_dp) / total[0:1, 0:1]

    fetches[6].wait()
    weight = turned[:, heads + 8:heads + 9]

    def forward_step(c, _):
        to_partner(xf_send, xf_recv, xfs, xfr, c).wait_recv()

        @pl.when(pair > 0)
        def _():
            to_pair(zf_send, zf_recv, zfs, zfr, c, me).wait_recv()

        own = xf_send[c, 0:state, :]
        own_keep = xf_send[c, state:state + 1, :]
        other = xf_recv[c, 0:state, :]
        other_keep = xf_recv[c, state:state + 1, :]
        entry = zf_recv[c]
        before = jnp.where(odd, other + other_keep * entry, entry)
        after = own + own_keep * before
        zf_send[c] = jnp.where(odd, after, other + other_keep * after)

        @pl.when(pair < pairs - 1)
        def _():
            to_pair(zf_send, zf_recv, zfs, zfr, c, me + 2).start()

        so_s[c] = after
        before_h = before.astype(BF16)
        rise = rise_s[c]
        y = rise * (y_s[c] + mm(queries_open, before_h))
        out_ref[:, lanes(c)] = y.astype(BF16)
        grad = weight * (y - t_ref[:, lanes(c)].astype(F32))
        z = (grad * rise).astype(BF16)
        xb_send[c] = mm(queries_t, z)
        to_partner(xb_send, xb_recv, xbs, xbr, c).start()
        y_s[c] = grad * y
        dq_s[...] += mm_nt(z, before_h)
        lifted = lift_s[c]
        dmix_s[...] += mm_nt(z, lifted)
        dmixt_s[...] += mm_nt(lifted, z)
        dl_s[c] = mm(mixing_t, z)
        return 0

    def backward_step(c, _):
        to_partner(xb_send, xb_recv, xbs, xbr, c).wait_recv()

        @pl.when(pair < pairs - 1)
        def _():
            to_pair(zb_send, zb_recv, zbs, zbr, c, me).wait_recv()

        own = xb_send[c]
        own_keep = xf_send[c, state:state + 1, :]
        other = xb_recv[c]
        other_keep = xf_recv[c, state:state + 1, :]
        entry = zb_recv[c]
        adjoint = jnp.where(odd, entry, other + other_keep * entry)
        onward = own + own_keep * adjoint
        zb_send[c] = jnp.where(odd, other + other_keep * onward, onward)

        @pl.when(pair > 0)
        def _():
            to_pair(zb_send, zb_recv, zbs, zbr, c, me - 2).start()

        e = spread(c)
        gain = rise_s[c, length - 1:length, :]
        adjoint = adjoint * over_mean
        scaled = (adjoint * (gain * sigma)).astype(BF16)
        d_feature = inv_s[c] * (dl_s[c] * over_mean + mm(keys_tail, scaled))
        gf_ref[:, lanes(c)] = d_feature.astype(BF16)
        change = y_s[c] * over_mean - f_ref[:, lanes(c)].astype(F32) * d_feature
        change_hi, change_lo = split(change)
        rt_s[...] += mm_nt(e, change_hi) + mm_nt(e, change_lo)
        dk_s[...] += mm_nt(lift_s[c], scaled)
        end_hi, end_lo = split(adjoint * so_s[c])
        ex_s[...] += mm_nt(e, end_hi) + mm_nt(e, end_lo)
        return 0

    def finish_scores():
        d_scores = (jnp.where(linked, dmix_s[...], 0.0) * (over_mean * sigma)).astype(BF16)
        d_scores_t = (jnp.where(linked_t, dmixt_s[...], 0.0) * (over_mean * sigma)).astype(BF16)
        gq_ref[...] = (mm(d_scores, keys) + (open_col * over_mean) * dq_s[...]).astype(BF16)
        gk_s[...] = mm(d_scores_t, queries)

    lag = jnp.minimum(chunks, LAG_LAST + LAG_PAIR * (pairs - 1 - pair))

    def step(i, _):
        @pl.when(i < chunks)
        def _():
            forward_step(i, 0)

        @pl.when(i == chunks)
        def _():
            finish_scores()

        @pl.when((i >= lag) & (i < lag + chunks))
        def _():
            backward_step(i - lag, 0)

        return 0

    lax.fori_loop(0, 2 * chunks, step, 0)

    gk_ref[...] = (gk_s[...] + tail_col * dk_s[...]).astype(BF16)
    rt_hi, rt_lo = split(rt_s[...])
    decay = mm(rt_hi, lower) + mm(rt_lo, lower) + jnp.sum(ex_s[...], axis=1, keepdims=True)
    gd_ref[...] = decay[:heads]

    def finish_step(c, _):
        to_partner(xf_send, xf_recv, xfs, xfr, c).wait_send()
        to_partner(xb_send, xb_recv, xbs, xbr, c).wait_send()

        @pl.when(pair < pairs - 1)
        def _():
            to_pair(zf_send, zf_recv, zfs, zfr, c, me + 2).wait_send()

        @pl.when(pair > 0)
        def _():
            to_pair(zb_send, zb_recv, zbs, zbr, c, me - 2).wait_send()

        return 0

    lax.fori_loop(0, chunks, finish_step, 0)

    def finish_w(d, _):
        w_seq(d).wait_send()
        return 0

    def finish_d(d, _):
        w_dp(d).wait_send()
        return 0

    lax.fori_loop(1, n_seq, finish_w, 0)
    lax.fori_loop(1, n_dp, finish_d, 0)


def body(features, key_proj, query_proj, log_decay, doc_start, loss_weight, target):
    n_seq, n_dp = lax.axis_size("seq"), lax.axis_size("dp")
    length, width = features.shape[1:]
    state = key_proj.shape[2]
    heads = log_decay.shape[1]
    chunks = width // CHUNK
    vmem = pl.BlockSpec(memory_space=pltpu.VMEM)
    big = (chunks, length, CHUNK)
    small = (chunks, state, CHUNK)
    padded = (chunks, state + EXTRA, CHUNK)
    scratch = [
        pltpu.VMEM(padded, F32), pltpu.VMEM(padded, F32),
        pltpu.VMEM(small, F32), pltpu.VMEM(small, F32),
        pltpu.VMEM(small, F32), pltpu.VMEM(small, F32),
        pltpu.VMEM(small, F32), pltpu.VMEM(small, F32),
        pltpu.VMEM(big, F32), pltpu.VMEM(big, F32), pltpu.VMEM(big, F32), pltpu.VMEM(big, F32),
        pltpu.VMEM(big, BF16), pltpu.VMEM(small, F32),
        pltpu.VMEM((length, length), F32), pltpu.VMEM((length, length), F32),
        pltpu.VMEM((length, state), F32), pltpu.VMEM((length, state), F32),
        pltpu.VMEM((length, state), F32), pltpu.VMEM((128, length), F32), pltpu.VMEM((128, state), F32),
        pltpu.VMEM((8, 128), F32), pltpu.VMEM((n_seq - 1, 8, 128), F32),
        pltpu.VMEM((8, 128), F32), pltpu.VMEM((n_dp - 1, 8, 128), F32),
    ]
    scratch += [
        pltpu.VMEM((length, width), BF16), pltpu.VMEM((length, state), BF16),
        pltpu.VMEM((length, state), BF16), pltpu.VMEM((heads, length), F32),
        pltpu.VMEM((1, length), jnp.int32), pltpu.VMEM((1, length), F32),
        pltpu.VMEM((length, width), BF16), pltpu.SemaphoreType.DMA((7,)),
    ]
    scratch += [pltpu.SemaphoreType.DMA((chunks,))] * 8
    scratch += [pltpu.SemaphoreType.DMA((n_seq - 1,))] * 2
    scratch += [pltpu.SemaphoreType.DMA((n_dp - 1,))] * 2
    results = pl.pallas_call(
        functools.partial(kernel, n_seq, n_dp, heads),
        out_shape=(
            jax.ShapeDtypeStruct((length, width), BF16),
            jax.ShapeDtypeStruct((length, width), BF16),
            jax.ShapeDtypeStruct((length, state), BF16),
            jax.ShapeDtypeStruct((length, state), BF16),
            jax.ShapeDtypeStruct((heads, length), F32),
        ),
        in_specs=[pl.BlockSpec(memory_space=pltpu.HBM)] * 7,
        out_specs=(vmem,) * 5,
        scratch_shapes=scratch,
        compiler_params=pltpu.CompilerParams(
            collective_id=0, has_side_effects=True, vmem_limit_bytes=60 << 20
        ),
        name="mixing",
    )(
        features[0], key_proj[0], query_proj[0], log_decay[0], doc_start, loss_weight, target[0]
    )
    return tuple(r[None] for r in results)


def solution(mesh):
    placed = (
        P("dp", "seq", None),
        P("dp", "seq", None),
        P("dp", "seq", None),
        P("dp", None, "seq"),
        P("dp", "seq"),
        P("dp", "seq"),
        P("dp", "seq", None),
    )
    return jax.shard_map(
        body,
        mesh=mesh,
        in_specs=placed,
        out_specs=(
            P("dp", "seq", None),
            P("dp", "seq", None),
            P("dp", "seq", None),
            P("dp", "seq", None),
            P("dp", None, "seq"),
        ),
        check_vma=False,
    )
```

```python
import functools
import math

import jax
import jax.numpy as jnp
from jax import lax
from jax.experimental import pallas as pl
from jax.experimental.pallas import tpu as pltpu
from jax.sharding import PartitionSpec as P

F32 = jnp.float32
BF16 = jnp.bfloat16
MESH = pl.DeviceIdType.MESH
CHUNK = 128
EXTRA = 8
LAG_LAST = 3
LAG_PAIR = 5


def mm(a, b):
    return jnp.dot(a, b, preferred_element_type=F32)


def mm_nt(a, b):
    return lax.dot_general(a, b, (((1,), (1,)), ((), ())), preferred_element_type=F32)


def split(x):
    hi = x.astype(BF16)
    lo = (x - hi.astype(F32)).astype(BF16)
    return hi, lo


def kernel(
    n_seq, n_dp, heads,
    f_hbm, k_hbm, q_hbm, ld_hbm, ds_hbm, w_hbm, t_hbm,
    out_ref, gf_ref, gk_ref, gq_ref, gd_ref,
    xf_send, xf_recv, zf_send, zf_recv, xb_send, xb_recv, zb_send, zb_recv,
    rise_s, inv_s, y_s, dl_s, lift_s, so_s,
    dmix_s, dmixt_s, dq_s, dk_s, gk_s, rt_s, ex_s,
    wown, wseq, wrow, wdp,
    f_ref, k_ref, q_ref, ld_ref, ds_ref, w_ref, t_ref, in_sem,
    xfs, xfr, zfs, zfr, xbs, xbr, zbs, zbr, wss, wsr, wds, wdr,
):
    length, width = f_ref.shape
    state = k_ref.shape[1]
    head_size = width // heads
    chunks = width // CHUNK
    per_chunk = CHUNK // head_size
    sigma = 1.0 / math.sqrt(state * length)

    me = lax.axis_index("seq")
    row = lax.axis_index("dp")
    pair = me // 2
    pairs = n_seq // 2
    is_odd = me % 2
    odd = is_odd == 1
    partner = me + 1 - 2 * is_odd

    fetches = [
        pltpu.make_async_copy(src, dst, in_sem.at[i])
        for i, (src, dst) in enumerate(
            [
                (ld_hbm, ld_ref), (ds_hbm, ds_ref), (w_hbm, w_ref), (k_hbm, k_ref),
                (q_hbm, q_ref), (f_hbm, f_ref), (t_hbm, t_ref),
            ]
        )
    ]
    for fetch in fetches:
        fetch.start()
    barrier = pltpu.get_barrier_semaphore()

    def greet_seq(d, _):
        pl.semaphore_signal(
            barrier, inc=1, device_id={"seq": (me + d) % n_seq}, device_id_type=MESH
        )
        return 0

    def greet_dp(d, _):
        pl.semaphore_signal(
            barrier, inc=1, device_id={"dp": (row + d) % n_dp}, device_id_type=MESH
        )
        return 0

    lax.fori_loop(1, n_seq, greet_seq, 0)
    lax.fori_loop(1, n_dp, greet_dp, 0)

    for fetch in fetches[:5]:
        fetch.wait()
    wown[...] = jnp.broadcast_to(jnp.sum(w_ref[...], axis=1, keepdims=True), wown.shape)

    starts = ds_ref[...].astype(F32)
    table = jnp.concatenate(
        [
            ld_ref[...],
            jnp.broadcast_to(starts, (8, length)),
            jnp.broadcast_to(w_ref[...], (8, length)),
            jnp.zeros((128 - heads - 16, length), F32),
        ],
        axis=0,
    )
    rows_i = lax.broadcasted_iota(jnp.int32, (length, length), 0)
    cols_i = lax.broadcasted_iota(jnp.int32, (length, length), 1)
    lower = (rows_i >= cols_i).astype(F32).astype(BF16)
    upper = (rows_i <= cols_i).astype(F32).astype(BF16)
    eye = (rows_i == cols_i).astype(F32).astype(BF16)
    eye_n = eye[:state, :state]
    table_hi, table_lo = split(table)
    cumulative = mm_nt(lower, table_hi) + mm_nt(lower, table_lo)
    turned = mm_nt(eye, table_hi) + mm_nt(eye, table_lo)
    seg_col = cumulative[:, heads:heads + 1]
    seg_row = mm(jnp.broadcast_to(starts, (8, length)).astype(BF16), upper)[0:1]
    last_seg = jnp.sum(starts, axis=1, keepdims=True)
    tail_row = (seg_row == last_seg).astype(F32)
    tail_col = (seg_col == last_seg).astype(F32)
    open_row = (seg_row == 0.0).astype(F32)
    open_col = (seg_col == 0.0).astype(F32)
    whole_block = (last_seg == 0.0).astype(F32)
    run_hi, run_lo = split(cumulative)

    keys = k_ref[...]
    queries = q_ref[...]
    keys_t = (mm_nt(eye_n, keys) * tail_row).astype(BF16)
    queries_t = (mm_nt(eye_n, queries) * open_row).astype(BF16)
    keys_tail = (keys.astype(F32) * tail_col).astype(BF16)
    queries_open = (queries.astype(F32) * open_col).astype(BF16)

    head_i = lax.broadcasted_iota(jnp.int32, (128, CHUNK), 0)
    lane_h = lax.broadcasted_iota(jnp.int32, (128, CHUNK), 1) // head_size

    def spread(c):
        return (head_i == lane_h + c * per_chunk).astype(F32).astype(BF16)

    def lanes(c):
        return pl.ds(pl.multiple_of(c * CHUNK, CHUNK), CHUNK)

    def to_partner(send, recv, ss, rs, c):
        return pltpu.make_async_remote_copy(
            src_ref=send.at[c], dst_ref=recv.at[c], send_sem=ss.at[c], recv_sem=rs.at[c],
            device_id={"seq": partner}, device_id_type=MESH,
        )

    def to_pair(send, recv, ss, rs, c, target):
        return pltpu.make_async_remote_copy(
            src_ref=send.at[c], dst_ref=recv.at[c], send_sem=ss.at[c], recv_sem=rs.at[c],
            device_id={"seq": target}, device_id_type=MESH,
        )

    def w_seq(d):
        return pltpu.make_async_remote_copy(
            src_ref=wown, dst_ref=wseq.at[d - 1], send_sem=wss.at[d - 1], recv_sem=wsr.at[d - 1],
            device_id={"seq": (me + d) % n_seq}, device_id_type=MESH,
        )

    def w_dp(d):
        return pltpu.make_async_remote_copy(
            src_ref=wrow, dst_ref=wdp.at[d - 1], send_sem=wds.at[d - 1], recv_sem=wdr.at[d - 1],
            device_id={"dp": (row + d) % n_dp}, device_id_type=MESH,
        )

    pl.semaphore_wait(barrier, n_seq + n_dp - 2)

    def start_w(d, _):
        w_seq(d).start()
        return 0

    def fresh_step(c, _):
        e = spread(c)
        run_x = mm(run_hi, e) + mm(run_lo, e)
        rise = jnp.exp(run_x)
        inv = jnp.exp(-run_x)
        lifted = (f_ref[:, lanes(c)].astype(F32) * inv).astype(BF16)
        gain = rise[length - 1:length]
        xf_send[c, 0:state, :] = mm(keys_t, lifted) * (gain * sigma)
        xf_send[c, state:state + EXTRA, :] = jnp.broadcast_to(gain * whole_block, (EXTRA, CHUNK))
        to_partner(xf_send, xf_recv, xfs, xfr, c).start()
        rise_s[c] = rise
        inv_s[c] = inv
        lift_s[c] = lifted
        return 0

    lax.fori_loop(1, n_seq, start_w, 0)
    fetches[5].wait()
    first = chunks // 4
    lax.fori_loop(0, first, fresh_step, 0)

    def add_w(d, total):
        w_seq(d).wait_recv()
        return total + wseq[d - 1]

    wrow[...] = lax.fori_loop(1, n_seq, add_w, wown[...])

    def start_d(d, _):
        w_dp(d).start()
        return 0

    lax.fori_loop(1, n_dp, start_d, 0)
    lax.fori_loop(first, chunks, fresh_step, 0)

    linked = (rows_i >= cols_i) & (seg_col == seg_row)
    linked_t = (rows_i <= cols_i) & (seg_col == seg_row)
    mixing = jnp.where(linked, mm_nt(queries, keys) * sigma, 0.0).astype(BF16)
    mixing_t = jnp.where(linked_t, mm_nt(keys, queries) * sigma, 0.0).astype(BF16)

    @pl.when(pair == 0)
    def _():
        zf_recv[...] = jnp.zeros_like(zf_recv)

    @pl.when(pair == pairs - 1)
    def _():
        zb_recv[...] = jnp.zeros_like(zb_recv)

    dmix_s[...] = jnp.zeros_like(dmix_s)
    dmixt_s[...] = jnp.zeros_like(dmixt_s)
    dq_s[...] = jnp.zeros_like(dq_s)
    dk_s[...] = jnp.zeros_like(dk_s)
    rt_s[...] = jnp.zeros_like(rt_s)
    ex_s[...] = jnp.zeros_like(ex_s)

    def inner_step(c, _):
        y_s[c] = mm(mixing, lift_s[c])
        return 0

    lax.fori_loop(0, chunks, inner_step, 0)

    def add_d(d, total):
        w_dp(d).wait_recv()
        return total + wdp[d - 1]

    total = lax.fori_loop(1, n_dp, add_d, wrow[...])
    over_mean = (length * n_seq * n_dp) / total[0:1, 0:1]

    fetches[6].wait()
    weight = turned[:, heads + 8:heads + 9]

    def forward_step(c, _):
        to_partner(xf_send, xf_recv, xfs, xfr, c).wait_recv()

        @pl.when(pair > 0)
        def _():
            to_pair(zf_send, zf_recv, zfs, zfr, c, me).wait_recv()

        own = xf_send[c, 0:state, :]
        own_keep = xf_send[c, state:state + 1, :]
        other = xf_recv[c, 0:state, :]
        other_keep = xf_recv[c, state:state + 1, :]
        entry = zf_recv[c]
        before = jnp.where(odd, other + other_keep * entry, entry)
        after = own + own_keep * before
        zf_send[c] = jnp.where(odd, after, other + other_keep * after)

        @pl.when(pair < pairs - 1)
        def _():
            to_pair(zf_send, zf_recv, zfs, zfr, c, me + 2).start()

        so_s[c] = after
        before_h = before.astype(BF16)
        rise = rise_s[c]
        y = rise * (y_s[c] + mm(queries_open, before_h))
        out_ref[:, lanes(c)] = y.astype(BF16)
        grad = weight * (y - t_ref[:, lanes(c)].astype(F32))
        z = (grad * rise).astype(BF16)
        xb_send[c] = mm(queries_t, z)
        to_partner(xb_send, xb_recv, xbs, xbr, c).start()
        y_s[c] = grad * y
        dq_s[...] += mm_nt(z, before_h)
        lifted = lift_s[c]
        dmix_s[...] += mm_nt(z, lifted)
        dmixt_s[...] += mm_nt(lifted, z)
        dl_s[c] = mm(mixing_t, z)
        return 0

    def backward_step(c, _):
        to_partner(xb_send, xb_recv, xbs, xbr, c).wait_recv()

        @pl.when(pair < pairs - 1)
        def _():
            to_pair(zb_send, zb_recv, zbs, zbr, c, me).wait_recv()

        own = xb_send[c]
        own_keep = xf_send[c, state:state + 1, :]
        other = xb_recv[c]
        other_keep = xf_recv[c, state:state + 1, :]
        entry = zb_recv[c]
        adjoint = jnp.where(odd, entry, other + other_keep * entry)
        onward = own + own_keep * adjoint
        zb_send[c] = jnp.where(odd, other + other_keep * onward, onward)

        @pl.when(pair > 0)
        def _():
            to_pair(zb_send, zb_recv, zbs, zbr, c, me - 2).start()

        e = spread(c)
        gain = rise_s[c, length - 1:length, :]
        adjoint = adjoint * over_mean
        scaled = (adjoint * (gain * sigma)).astype(BF16)
        d_feature = inv_s[c] * (dl_s[c] * over_mean + mm(keys_tail, scaled))
        gf_ref[:, lanes(c)] = d_feature.astype(BF16)
        change = y_s[c] * over_mean - f_ref[:, lanes(c)].astype(F32) * d_feature
        change_hi, change_lo = split(change)
        rt_s[...] += mm_nt(e, change_hi) + mm_nt(e, change_lo)
        dk_s[...] += mm_nt(lift_s[c], scaled)
        end_hi, end_lo = split(adjoint * so_s[c])
        ex_s[...] += mm_nt(e, end_hi) + mm_nt(e, end_lo)
        return 0

    def finish_scores():
        d_scores = (jnp.where(linked, dmix_s[...], 0.0) * (over_mean * sigma)).astype(BF16)
        d_scores_t = (jnp.where(linked_t, dmixt_s[...], 0.0) * (over_mean * sigma)).astype(BF16)
        gq_ref[...] = (mm(d_scores, keys) + (open_col * over_mean) * dq_s[...]).astype(BF16)
        gk_s[...] = mm(d_scores_t, queries)

    lag = jnp.minimum(chunks, LAG_LAST + LAG_PAIR * (pairs - 1 - pair))

    def step(i, _):
        @pl.when(i < chunks)
        def _():
            forward_step(i, 0)

        @pl.when(i == chunks)
        def _():
            finish_scores()

        @pl.when((i >= lag) & (i < lag + chunks))
        def _():
            backward_step(i - lag, 0)

        return 0

    lax.fori_loop(0, 2 * chunks, step, 0)

    gk_ref[...] = (gk_s[...] + tail_col * dk_s[...]).astype(BF16)
    rt_hi, rt_lo = split(rt_s[...])
    decay = mm(rt_hi, lower) + mm(rt_lo, lower) + jnp.sum(ex_s[...], axis=1, keepdims=True)
    gd_ref[...] = decay[:heads]

    def finish_step(c, _):
        to_partner(xf_send, xf_recv, xfs, xfr, c).wait_send()
        to_partner(xb_send, xb_recv, xbs, xbr, c).wait_send()

        @pl.when(pair < pairs - 1)
        def _():
            to_pair(zf_send, zf_recv, zfs, zfr, c, me + 2).wait_send()

        @pl.when(pair > 0)
        def _():
            to_pair(zb_send, zb_recv, zbs, zbr, c, me - 2).wait_send()

        return 0

    lax.fori_loop(0, chunks, finish_step, 0)

    def finish_w(d, _):
        w_seq(d).wait_send()
        return 0

    def finish_d(d, _):
        w_dp(d).wait_send()
        return 0

    lax.fori_loop(1, n_seq, finish_w, 0)
    lax.fori_loop(1, n_dp, finish_d, 0)


def body(features, key_proj, query_proj, log_decay, doc_start, loss_weight, target):
    n_seq, n_dp = lax.axis_size("seq"), lax.axis_size("dp")
    length, width = features.shape[1:]
    state = key_proj.shape[2]
    heads = log_decay.shape[1]
    chunks = width // CHUNK
    vmem = pl.BlockSpec(memory_space=pltpu.VMEM)
    big = (chunks, length, CHUNK)
    small = (chunks, state, CHUNK)
    padded = (chunks, state + EXTRA, CHUNK)
    scratch = [
        pltpu.VMEM(padded, F32), pltpu.VMEM(padded, F32),
        pltpu.VMEM(small, F32), pltpu.VMEM(small, F32),
        pltpu.VMEM(small, F32), pltpu.VMEM(small, F32),
        pltpu.VMEM(small, F32), pltpu.VMEM(small, F32),
        pltpu.VMEM(big, F32), pltpu.VMEM(big, F32), pltpu.VMEM(big, F32), pltpu.VMEM(big, F32),
        pltpu.VMEM(big, BF16), pltpu.VMEM(small, F32),
        pltpu.VMEM((length, length), F32), pltpu.VMEM((length, length), F32),
        pltpu.VMEM((length, state), F32), pltpu.VMEM((length, state), F32),
        pltpu.VMEM((length, state), F32), pltpu.VMEM((128, length), F32), pltpu.VMEM((128, state), F32),
        pltpu.VMEM((8, 128), F32), pltpu.VMEM((n_seq - 1, 8, 128), F32),
        pltpu.VMEM((8, 128), F32), pltpu.VMEM((n_dp - 1, 8, 128), F32),
    ]
    scratch += [
        pltpu.VMEM((length, width), BF16), pltpu.VMEM((length, state), BF16),
        pltpu.VMEM((length, state), BF16), pltpu.VMEM((heads, length), F32),
        pltpu.VMEM((1, length), jnp.int32), pltpu.VMEM((1, length), F32),
        pltpu.VMEM((length, width), BF16), pltpu.SemaphoreType.DMA((7,)),
    ]
    scratch += [pltpu.SemaphoreType.DMA((chunks,))] * 8
    scratch += [pltpu.SemaphoreType.DMA((n_seq - 1,))] * 2
    scratch += [pltpu.SemaphoreType.DMA((n_dp - 1,))] * 2
    results = pl.pallas_call(
        functools.partial(kernel, n_seq, n_dp, heads),
        out_shape=(
            jax.ShapeDtypeStruct((length, width), BF16),
            jax.ShapeDtypeStruct((length, width), BF16),
            jax.ShapeDtypeStruct((length, state), BF16),
            jax.ShapeDtypeStruct((length, state), BF16),
            jax.ShapeDtypeStruct((heads, length), F32),
        ),
        in_specs=[pl.BlockSpec(memory_space=pltpu.HBM)] * 7,
        out_specs=(vmem,) * 5,
        scratch_shapes=scratch,
        compiler_params=pltpu.CompilerParams(
            collective_id=0, has_side_effects=True, vmem_limit_bytes=60 << 20
        ),
        name="mixing",
    )(
        features[0], key_proj[0], query_proj[0], log_decay[0], doc_start, loss_weight, target[0]
    )
    return tuple(r[None] for r in results)


def solution(mesh):
    placed = (
        P("dp", "seq", None),
        P("dp", "seq", None),
        P("dp", "seq", None),
        P("dp", None, "seq"),
        P("dp", "seq"),
        P("dp", "seq"),
        P("dp", "seq", None),
    )
    return jax.shard_map(
        body,
        mesh=mesh,
        in_specs=placed,
        out_specs=(
            P("dp", "seq", None),
            P("dp", "seq", None),
            P("dp", "seq", None),
            P("dp", "seq", None),
            P("dp", None, "seq"),
        ),
        check_vma=False,
    )
```
